128 devices in a mesh: gx: 8 (over z_hi, y), gy: 4 (over x), gz: 4 (over z_lo, core).
Axes of the slice: x: 4, y: 4, z: 4 (z_hi: 2, z_lo: 2; z = z_hi * 2 + z_lo), core: 2. Of those that a mesh axis runs over, the one named last changes fastest.
Arguments:
- bold_data: bfloat16 [64, 64, 128, 512], P('gx', 'gy', 'gz'), may hold values from -6 to 6
- spatial_maps: float32 [64, 64, 64, 128], P(None, 'gx', 'gy', 'gz'), may hold values from -6 to 6
- live_blocks: int32 [8, 4, 4], P('gx', 'gy', 'gz'), may hold values from 16 to 128, as said below
Outputs:
- new_maps: float32 [64, 64, 64, 128], P(None, 'gx', 'gy', 'gz')
- time_courses: bfloat16 [64, 512], replicated
The draws below stay inside these ranges and needn't reach their ends.
Inputs may be any that keep to these rules, and one draw needn't show every extreme that they name: live_blocks counts live rows of a device's block; rows are numbered (x mod 8) * 16 + (y mod 16) and the live ones come first.
All inputs are finite; a program needn't handle non-finite values.
Results may differ from the reference program's by a relative error of at most 0.011.
Values may be sent and summed in bfloat16 or wider, within the bound.
A program may use at most 192 MiB of HBM per device.

```python
import math
import jax
import jax.numpy as jnp
from jax import lax

K = 64
FRAMES = 512
RADIUS = 8
ITERS = 2
CX = 8
CY = 16
CZ = 32
NX = 64
NY = 64
NZ = 128
N_GX = 8
N_GY = 4
N_GZ = 4


def draw_live_blocks(key, part):
    first, second = jax.random.split(key)
    total = N_GX * N_GY * N_GZ
    values = jax.random.randint(first, (total,), CX * CY // 8, CX * CY + 1)
    picked = jax.random.randint(second, (), 0, total)
    values = jnp.where(jnp.arange(total) == picked, CX * CY, values)
    return values.reshape(N_GX, N_GY, N_GZ).astype(jnp.int32)


def steps_of(key, extent, shards, low, top_value):
    gain = 1.0
    for axis_at, parts in shards:
        steps = jax.random.uniform(jax.random.fold_in(jax.random.fold_in(key, 6), axis_at), (parts,), jnp.float32, low / len(shards), top_value / len(shards))
        gain = gain * jnp.repeat(jnp.exp(steps), extent[axis_at] // parts).reshape((-1,) + (1,) * (len(extent) - 1 - axis_at))
    return gain


def normal_values(key, dims, scale, most, cuts=(), kind=jnp.bfloat16):
    factor_of = steps_of(key, dims, cuts, -0.22, 0.18) if cuts else 1.0
    array = jax.random.normal(key, dims, jnp.float32) * scale * factor_of
    return jnp.minimum(jnp.maximum(array, -most), most).astype(kind)


def setup_inputs(seed: int = 0) -> dict:
    key_of = jax.random.split(jax.random.key(seed), 4)
    bold_data = normal_values(key_of[0], (NX, NY, NZ, FRAMES), 1.0, 6.0, ((0, 8), (1, 4), (2, 4)))
    spatial_maps = normal_values(key_of[1], (K, NX, NY, NZ), 1.0, 6.0, ((1, 8), (2, 4), (3, 4)), jnp.float32)
    live_blocks = draw_live_blocks(jax.random.fold_in(key_of[3], 71), 0)
    return dict(bold_data=bold_data, spatial_maps=spatial_maps, live_blocks=live_blocks)


def band_matrix(length, dtype):
    total = sum((math.exp(-float(d * d) / 32.0) for d in range(-RADIUS, RADIUS + 1)))
    count = length - 2 * RADIUS
    rows = lax.broadcasted_iota(jnp.int32, (length, count), 0)
    cols = lax.broadcasted_iota(jnp.int32, (length, count), 1)
    offset = (rows - cols - RADIUS).astype(dtype)
    inside = jnp.logical_and(rows - cols >= 0, rows - cols <= 2 * RADIUS)
    return jnp.where(inside, jnp.exp(-offset * offset / 32.0) / total, jnp.zeros_like(offset))

def filter_along(field, axis):
    band = band_matrix(field.shape[axis], field.dtype)
    result = jnp.tensordot(field, band, axes=((axis,), (0,)), precision=lax.Precision.HIGHEST)
    return jnp.moveaxis(result, -1, axis)

def smooth_one(single):
    padded = jnp.pad(single.astype(jnp.float32), RADIUS)
    return filter_along(filter_along(filter_along(padded, 0), 1), 2)

def reference(bold_data, spatial_maps, live_blocks):
    rows = (jnp.arange(NX, dtype=jnp.int32) % CX)[:, None] * CY + (jnp.arange(NY, dtype=jnp.int32) % CY)[None, :]
    counts = jnp.repeat(jnp.repeat(jnp.repeat(live_blocks, CX, axis=0), CY, axis=1), CZ, axis=2)
    live = rows[:, :, None] < counts
    live_half = live.astype(jnp.bfloat16)[None]
    live_flat = live.reshape(-1).astype(jnp.float32)
    flat_frames = bold_data.reshape(NX * NY * NZ, FRAMES)
    weights = spatial_maps.reshape(K, NX * NY * NZ)
    rounded = None
    for step in range(ITERS):
        plain = weights.reshape(K, NX, NY, NZ).astype(jnp.bfloat16)
        smoothed = lax.map(smooth_one, plain).astype(jnp.bfloat16) * live_half
        courses = jnp.dot(smoothed.reshape(K, -1), flat_frames, preferred_element_type=jnp.float32)
        gram = jnp.dot(courses, courses.T, precision=lax.Precision.HIGHEST)
        trace_value = jnp.trace(gram)
        rounded = courses.astype(jnp.bfloat16)
        raw_grad = (jnp.dot(rounded, flat_frames.T, preferred_element_type=jnp.float32) * live_flat[None, :]).astype(jnp.bfloat16)
        grad = lax.map(smooth_one, raw_grad.reshape(K, NX, NY, NZ)).reshape(K, -1)
        energy = jnp.sum(grad * grad) / float(K * NX * NY * NZ)
        scale = 1.0 / jnp.sqrt(energy + 1e-06)
        decay = jnp.dot(gram, weights, precision=lax.Precision.HIGHEST)
        weights = weights + 0.5 * (grad * scale - float(K) / trace_value * decay)
    return (weights.reshape(K, NX, NY, NZ), rounded)
```

```python
import functools
import math

import jax
import jax.numpy as jnp
import numpy as np
from jax import lax
from jax.experimental import pallas as pl
from jax.experimental.pallas import tpu as pltpu
from jax.sharding import PartitionSpec as P

MESH = pl.DeviceIdType.MESH
RADIUS = 8
K, T = 64, 512
BX, BY, BZ = 8, 16, 32
YZ = BY * BZ
CH = 16
NC = K // CH
ROWS = BX * CH
F32, BF16 = jnp.float32, jnp.bfloat16
HIGH = lax.Precision.HIGHEST


def tap_of(offset):
    total = sum(math.exp(-float(d * d) / 32.0) for d in range(-RADIUS, RADIUS + 1))
    taps = np.exp(-np.square(np.asarray(offset, np.float64)) / 32.0) / total
    return np.where(np.abs(offset) <= RADIUS, taps, 0.0)


def filter_matrices():
    col = np.arange(YZ)
    col_y, col_z = col // BZ, col % BZ
    edge = np.arange(2 * BY * RADIUS)
    edge_y = (edge % (BY * RADIUS)) // RADIUS
    low = edge < BY * RADIUS
    edge_z = np.where(low, edge % RADIUS, BZ - RADIUS + edge % RADIUS)
    pack = (col_y[:, None] == edge_y[None]) & (col_z[:, None] == edge_z[None])
    half_y, half_z = col_y[: YZ // 2], col_z[: YZ // 2]
    own_z = (half_y[:, None] == half_y[None]) * tap_of(half_z[:, None] - half_z[None])
    from_z = np.where(low, edge % RADIUS - RADIUS, BZ + edge % RADIUS)
    edges_z = (edge_y[:, None] == col_y[None]) * tap_of(from_z[:, None] - col_z[None])
    row = np.arange(2 * YZ)
    row_y = np.where(row < YZ, row // BZ, np.where(row < YZ * 3 // 2, (row - YZ) // BZ - RADIUS, (row - YZ) // BZ - RADIUS + BY))
    full_y = ((row % BZ)[:, None] == col_z[None]) * tap_of(row_y[:, None] - col_y[None])
    out = np.arange(ROWS)
    src = np.arange(3 * ROWS)
    full_x = ((src % CH)[None] == (out % CH)[:, None]) * tap_of((src // CH - BX)[None] - (out // CH)[:, None])
    return [jnp.asarray(m, BF16) for m in (pack, own_z, edges_z, full_y, full_x)]


def kernel(
    nx, ny, nz,
    live_ref, plain_hbm, w_hbm, x_hbm, pack_hbm, ownz_hbm, edgez_hbm, fully_hbm, fullx_hbm,
    out_ref, tc_ref,
    src, wmap, xdat, pack, ownz, edgez, fully, fullx,
    zpack, fz, fyz, smooth, ze, ye, xe, grad, mixed,
    cpart, c1, c2, rz, ry, rx, etot, ez, ey, ex,
    load_sem, hs, hr, az_s, az_r, ay_s, ay_r, ax_s, ax_r, gy_s, gy_r, gz_s, gz_r,
    es_z, er_z, es_y, er_y, es_x, er_x,
):
    ix, iy, iz = lax.axis_index("gx"), lax.axis_index("gy"), lax.axis_index("gz")
    rows_z, lanes_y = K // nz, T // ny
    cells = float(K * BX * BY * BZ * nx * ny * nz)

    loads = [
        pltpu.make_async_copy(a, b, load_sem.at[i])
        for i, (a, b) in enumerate(
            [(plain_hbm, src), (pack_hbm, pack), (ownz_hbm, ownz), (edgez_hbm, edgez), (fully_hbm, fully),
             (fullx_hbm, fullx), (x_hbm, xdat), (w_hbm, wmap)]
        )
    ]
    for load in loads:
        load.start()

    barrier = pltpu.get_barrier_semaphore()
    for name, me, n in (("gx", ix, nx), ("gy", iy, ny), ("gz", iz, nz)):
        for d in range(1, n):
            pl.semaphore_signal(barrier, inc=1, device_id={name: lax.rem(me + d, n)}, device_id_type=MESH)

    @pl.when(ix == 0)
    def _():
        xe[:, 0] = jnp.zeros_like(xe[:, 0])

    @pl.when(ix == nx - 1)
    def _():
        xe[:, 1] = jnp.zeros_like(xe[:, 1])

    @pl.when(iy == 0)
    def _():
        ye[:, :, :, : YZ // 2] = jnp.zeros_like(ye[:, :, :, : YZ // 2])

    @pl.when(iy == ny - 1)
    def _():
        ye[:, :, :, YZ // 2 :] = jnp.zeros_like(ye[:, :, :, YZ // 2 :])

    @pl.when(iz == 0)
    def _():
        ze[:, :, :, :128] = jnp.zeros_like(ze[:, :, :, :128])

    @pl.when(iz == nz - 1)
    def _():
        ze[:, :, :, 128:] = jnp.zeros_like(ze[:, :, :, 128:])

    pl.semaphore_wait(barrier, nx + ny + nz - 3)
    loads[0].wait()
    loads[1].wait()

    def dot(a, b):
        return jnp.dot(a, b, preferred_element_type=F32)

    def maps(c):
        return pl.ds(pl.multiple_of(c * CH, CH), CH)

    def halo(s, c, axis):
        k = maps(c)

        def copy(i, a, b, axis, to):
            return pltpu.make_async_remote_copy(
                src_ref=a, dst_ref=b, send_sem=hs.at[s, c, i], recv_sem=hr.at[s, c, i],
                device_id={axis: to}, device_id_type=MESH,
            )

        half = YZ // 2
        if axis == "z":
            down = (0, zpack.at[:, k, pl.ds(0, 128)], ze.at[s, :, k, pl.ds(128, 128)])
            up = (1, zpack.at[:, k, pl.ds(128, 128)], ze.at[s, :, k, pl.ds(0, 128)])
            name, me, n = "gz", iz, nz
        elif axis == "y":
            down = (2, fz.at[:, k, pl.ds(0, half)], ye.at[s, :, k, pl.ds(half, half)])
            up = (3, fz.at[:, k, pl.ds(half, half)], ye.at[s, :, k, pl.ds(0, half)])
            name, me, n = "gy", iy, ny
        else:
            down = (4, fyz.at[:, k, :], xe.at[s, 1, :, k, :])
            up = (5, fyz.at[:, k, :], xe.at[s, 0, :, k, :])
            name, me, n = "gx", ix, nx
        return (
            (me > 0, me < n - 1, copy(*down, name, lax.rem(me + n - 1, n))),
            (me < n - 1, me > 0, copy(*up, name, lax.rem(me + 1, n))),
        )

    def send(s, c, axis):
        for sends, _, copy in halo(s, c, axis):
            @pl.when(sends)
            def _():
                copy.start()

    def receive(s, c, axis):
        for _, comes, copy in halo(s, c, axis):
            @pl.when(comes)
            def _():
                copy.wait_recv()

    def sent(s, c):
        for axis in "zyx":
            for sends, _, copy in halo(s, c, axis):
                @pl.when(sends)
                def _():
                    copy.wait_send()

    count = live_ref[0, 0, 0]
    row_y = lax.broadcasted_iota(jnp.int32, (1, YZ), 1) // BZ

    def chunks(body):
        lax.fori_loop(0, NC, lambda c, _: (body(c), 0)[1], 0)

    def smoothing(s, finish):
        def pack_z(c):
            k = maps(c)
            zpack[:, k, :] = dot(src[:, k, :].reshape(ROWS, YZ), pack[...]).astype(BF16).reshape(BX, CH, 2 * 128)
            send(s, c, "z")

        def filter_z(c):
            k = maps(c)
            receive(s, c, "z")
            field = src[:, k, :].reshape(ROWS, YZ)
            own = jnp.concatenate([dot(field[:, : YZ // 2], ownz[...]), dot(field[:, YZ // 2 :], ownz[...])], axis=1)
            edges = dot(ze[s, :, k, :].reshape(ROWS, 2 * 128), edgez[...])
            fz[:, k, :] = (own + edges).astype(BF16).reshape(BX, CH, YZ)
            send(s, c, "y")

        def filter_y(c):
            k = maps(c)
            receive(s, c, "y")
            field = jnp.concatenate([fz[:, k, :].reshape(ROWS, YZ), ye[s, :, k, :].reshape(ROWS, YZ)], axis=1)
            fyz[:, k, :] = dot(field, fully[...]).astype(BF16).reshape(BX, CH, YZ)
            send(s, c, "x")

        def filter_x(c):
            k = maps(c)
            receive(s, c, "x")
            field = jnp.concatenate(
                [xe[s, 0, :, k, :].reshape(ROWS, YZ), fyz[:, k, :].reshape(ROWS, YZ), xe[s, 1, :, k, :].reshape(ROWS, YZ)],
                axis=0,
            )
            finish(c, dot(fullx[...], field).reshape(BX, CH, YZ))

        chunks(pack_z)
        if s == 0:
            loads[2].wait()
            loads[3].wait()
        chunks(filter_z)
        if s == 0:
            loads[4].wait()
        chunks(filter_y)
        if s == 0:
            loads[5].wait()
        return filter_x

    def end_of(s):
        chunks(lambda c: sent(s, c))

    def mask_of(x):
        return x * BY + row_y < count

    def finish_smooth(c, value):
        k = maps(c)
        for x in range(BX):
            smooth[x, k, :] = jnp.where(mask_of(x), value[x], 0.0).astype(BF16)

    def finish_grad(c, value):
        grad[:, maps(c), :] = value
        src[:, maps(c), :] = value.astype(BF16)

    def finish_last(c, value):
        out_ref[:, maps(c), :] = value

    def square_sum(ref):
        def body(x, total):
            return total + ref[x] * ref[x]

        return jnp.sum(lax.fori_loop(0, BX, body, jnp.zeros((K, YZ), F32)))

    def contribution():
        total = dot(smooth[0], xdat[pl.ds(0, YZ), :])
        for x in range(1, BX):
            total += dot(smooth[x], xdat[pl.ds(x * YZ, YZ), :])
        return total

    def gradient(courses):
        for x in range(BX):
            value = lax.dot_general(
                courses, xdat[pl.ds(x * YZ, YZ), :], (((1,), (1,)), ((), ())), preferred_element_type=F32
            )
            src[x] = jnp.where(mask_of(x), value, 0.0).astype(BF16)

    def remote(a, b, ssem, rsem, axis, to):
        return pltpu.make_async_remote_copy(
            src_ref=a, dst_ref=b, send_sem=ssem, recv_sem=rsem, device_id={axis: to}, device_id_type=MESH
        )

    def swap(axis, me, n, piece, slots, ssem, rsem):
        copies = []
        for d in range(1, n):
            to = lax.rem(me + d, n)
            copy = remote(piece(to), slots.at[me], ssem.at[d - 1], rsem.at[me], axis, to)
            copy.start()
            copies.append(copy)
        for d in range(1, n):
            come = lax.rem(me + d, n)
            remote(piece(come), slots.at[come], ssem.at[d - 1], rsem.at[come], axis, come).wait_recv()
        return copies

    def sum_slots(slots, n):
        total = slots[0]
        for j in range(1, n):
            total += slots[j]
        return total

    def all_reduce(a, extra, result):
        height = rows_z + 8
        copies = swap("gz", iz, nz, lambda j: cpart.at[j], rz.at[a], az_s.at[a], az_r.at[a])
        rz[a, iz] = cpart[iz]
        part = sum_slots(rz.at[a], nz)
        for j in range(ny):
            ry[a, ny + j] = part[:, j * lanes_y : (j + 1) * lanes_y]
        copies += swap("gy", iy, ny, lambda j: ry.at[a, ny + j], ry.at[a], ay_s.at[a], ay_r.at[a])
        ry[a, iy] = ry[a, ny + iy]
        rx[a, nx] = sum_slots(ry.at[a], ny)
        copies += swap("gx", ix, nx, lambda j: rx.at[a, nx], rx.at[a], ax_s.at[a], ax_r.at[a])
        rx[a, ix] = rx[a, nx]
        total = sum_slots(rx.at[a], nx)
        etot[...] = total[rows_z:, :128]
        rows = pl.ds(pl.multiple_of(iz * rows_z, rows_z), rows_z)
        lanes = pl.ds(pl.multiple_of(iy * lanes_y, lanes_y), lanes_y)
        result[rows, lanes] = total[:rows_z]
        for d in range(1, ny):
            to = lax.rem(iy + d, ny)
            copy = remote(result.at[rows, lanes], result.at[rows, lanes], gy_s.at[a, d - 1], gy_r.at[a, iy], "gy", to)
            copy.start()
            copies.append(copy)
        for d in range(1, ny):
            come = lax.rem(iy + d, ny)
            there = result.at[rows, pl.ds(pl.multiple_of(come * lanes_y, lanes_y), lanes_y)]
            remote(there, there, gy_s.at[a, d - 1], gy_r.at[a, come], "gy", come).wait_recv()
        for d in range(1, nz):
            to = lax.rem(iz + d, nz)
            copy = remote(result.at[rows, :], result.at[rows, :], gz_s.at[a, d - 1], gz_r.at[a, iz], "gz", to)
            copy.start()
            copies.append(copy)
        for d in range(1, nz):
            come = lax.rem(iz + d, nz)
            there = result.at[pl.ds(pl.multiple_of(come * rows_z, rows_z), rows_z), :]
            remote(there, there, gz_s.at[a, d - 1], gz_r.at[a, come], "gz", come).wait_recv()
        for copy in copies:
            copy.wait_send()

    def fill_cpart(value, energy):
        for j in range(nz):
            cpart[j, :rows_z] = value[j * rows_z : (j + 1) * rows_z]
            cpart[j, rows_z:] = jnp.full((8, T), energy, F32)

    def gram_of(courses):
        gram = lax.dot_general(courses, courses, (((1,), (1,)), ((), ())), precision=HIGH, preferred_element_type=F32)
        diag = lax.broadcasted_iota(jnp.int32, (K, K), 0) == lax.broadcasted_iota(jnp.int32, (K, K), 1)
        return gram, jnp.sum(jnp.where(diag, gram, 0.0))

    def exact(a, b):
        return jnp.dot(a, b, precision=HIGH, preferred_element_type=F32)

    last = smoothing(0, finish_smooth)
    loads[6].wait()
    chunks(last)
    end_of(0)
    fill_cpart(contribution(), 0.0)
    all_reduce(0, None, c1)
    gradient(c1[...].astype(BF16))
    last = smoothing(1, finish_grad)
    gram1, trace1 = gram_of(c1[...])
    decay1 = float(K) / trace1 * gram1
    loads[7].wait()
    chunks(last)
    end_of(1)
    energy1 = square_sum(grad)
    last = smoothing(2, finish_smooth)
    for x in range(BX):
        mixed[x] = wmap[x] - 0.5 * exact(decay1, wmap[x])
    chunks(last)
    end_of(2)
    fill_cpart(contribution(), energy1)
    all_reduce(1, None, c2)
    scale1 = 1.0 / jnp.sqrt(etot[0:1, 0:1] / cells + 1e-06)
    c2[...] = c1[...] + 0.5 * (scale1 * c2[...] - exact(decay1, c1[...]))
    tc_ref[...] = c2[...].astype(BF16)
    gradient(c2[...].astype(BF16))
    last = smoothing(3, finish_last)
    gram2, trace2 = gram_of(c2[...])
    decay2 = float(K) / trace2 * gram2
    for x in range(BX):
        now = mixed[x] + 0.5 * scale1 * grad[x]
        mixed[x] = now - 0.5 * exact(decay2, now)
    chunks(last)
    end_of(3)
    etot[...] = jnp.full((8, 128), square_sum(out_ref), F32)
    copies = []
    for axis, me, n, slots, ssem, rsem in (
        ("gz", iz, nz, ez, es_z, er_z), ("gy", iy, ny, ey, es_y, er_y), ("gx", ix, nx, ex, es_x, er_x)
    ):
        slots[n] = etot[...]
        copies += swap(axis, me, n, lambda j: slots.at[n], slots, ssem, rsem)
        slots[me] = slots[n]
        etot[...] = sum_slots(slots, n)
    scale2 = 1.0 / jnp.sqrt(etot[0:1, 0:1] / cells + 1e-06)
    for x in range(BX):
        out_ref[x] = mixed[x] + 0.5 * scale2 * out_ref[x]
    for copy in copies:
        copy.wait_send()


def per_device(nx, ny, nz, bold_data, spatial_maps, live_blocks):
    rows_z, lanes_y = K // nz, T // ny
    planes = jnp.transpose(spatial_maps, (1, 0, 2, 3)).reshape(BX, K, YZ)
    matrices = filter_matrices()
    vmem, dma = pltpu.VMEM, pltpu.SemaphoreType.DMA
    field = vmem((BX, K, YZ), BF16)
    new_maps, courses = pl.pallas_call(
        functools.partial(kernel, nx, ny, nz),
        out_shape=(jax.ShapeDtypeStruct((BX, K, YZ), F32), jax.ShapeDtypeStruct((K, T), BF16)),
        in_specs=[pl.BlockSpec(memory_space=pltpu.SMEM)] + [pl.BlockSpec(memory_space=pl.ANY)] * 8,
        out_specs=(pl.BlockSpec(memory_space=pltpu.VMEM), pl.BlockSpec(memory_space=pltpu.VMEM)),
        scratch_shapes=[
            field, vmem((BX, K, YZ), F32), vmem((BX * YZ, T), BF16),
            *[vmem(m.shape, BF16) for m in matrices],
            vmem((BX, K, 256), BF16), field, field, field,
            vmem((4, BX, K, 256), BF16), vmem((4, BX, K, YZ), BF16), vmem((4, 2, BX, K, YZ), BF16),
            vmem((BX, K, YZ), F32), vmem((BX, K, YZ), F32),
            vmem((nz, rows_z + 8, T), F32), vmem((K, T), F32), vmem((K, T), F32),
            vmem((2, nz, rows_z + 8, T), F32),
            vmem((2, 2 * ny, rows_z + 8, lanes_y), F32),
            vmem((2, nx + 1, rows_z + 8, lanes_y), F32),
            vmem((8, 128), F32), vmem((nz + 1, 8, 128), F32), vmem((ny + 1, 8, 128), F32), vmem((nx + 1, 8, 128), F32),
            dma((8,)), dma((4, NC, 6)), dma((4, NC, 6)),
            dma((2, nz)), dma((2, nz)), dma((2, ny)), dma((2, ny)), dma((2, nx)), dma((2, nx)),
            dma((2, ny)), dma((2, ny)), dma((2, nz)), dma((2, nz)),
            dma((nz,)), dma((nz,)), dma((ny,)), dma((ny,)), dma((nx,)), dma((nx,)),
        ],
        compiler_params=pltpu.CompilerParams(
            collective_id=0, has_side_effects=True, vmem_limit_bytes=56 * 1024 * 1024
        ),
    )(live_blocks, planes.astype(BF16), planes, bold_data.reshape(BX * YZ, T), *matrices)
    new_maps = jnp.transpose(new_maps.reshape(BX, K, BY, BZ), (1, 0, 2, 3))
    return new_maps, courses


def solution(mesh):
    return jax.shard_map(
        functools.partial(per_device, mesh.shape["gx"], mesh.shape["gy"], mesh.shape["gz"]),
        mesh=mesh,
        in_specs=(P("gx", "gy", "gz", None), P(None, "gx", "gy", "gz"), P("gx", "gy", "gz")),
        out_specs=(P(None, "gx", "gy", "gz"), P()),
        check_vma=False,
    )
```

```python
import functools
import math

import jax
import jax.numpy as jnp
import numpy as np
from jax import lax
from jax.experimental import pallas as pl
from jax.experimental.pallas import tpu as pltpu
from jax.sharding import PartitionSpec as P

MESH = pl.DeviceIdType.MESH
RADIUS = 8
K, T = 64, 512
BX, BY, BZ = 8, 16, 32
YZ = BY * BZ
CH = 16
NC = K // CH
PAIR = 2
PR, NP = PAIR * CH, NC // PAIR
ROWS = BX * CH
F32, BF16 = jnp.float32, jnp.bfloat16
HIGH = lax.Precision.HIGHEST


def tap_of(offset):
    total = sum(math.exp(-float(d * d) / 32.0) for d in range(-RADIUS, RADIUS + 1))
    taps = np.exp(-np.square(np.asarray(offset, np.float64)) / 32.0) / total
    return np.where(np.abs(offset) <= RADIUS, taps, 0.0)


def filter_matrices():
    col = np.arange(YZ)
    col_y, col_z = col // BZ, col % BZ
    edge = np.arange(2 * BY * RADIUS)
    edge_y = (edge % (BY * RADIUS)) // RADIUS
    low = edge < BY * RADIUS
    edge_z = np.where(low, edge % RADIUS, BZ - RADIUS + edge % RADIUS)
    pack = (col_y[:, None] == edge_y[None]) & (col_z[:, None] == edge_z[None])
    half_y, half_z = col_y[: YZ // 2], col_z[: YZ // 2]
    own_z = (half_y[:, None] == half_y[None]) * tap_of(half_z[:, None] - half_z[None])
    from_z = np.where(low, edge % RADIUS - RADIUS, BZ + edge % RADIUS)
    edges_z = (edge_y[:, None] == col_y[None]) * tap_of(from_z[:, None] - col_z[None])
    row = np.arange(2 * YZ)
    row_y = np.where(row < YZ, row // BZ, np.where(row < YZ * 3 // 2, (row - YZ) // BZ - RADIUS, (row - YZ) // BZ - RADIUS + BY))
    full_y = ((row % BZ)[:, None] == col_z[None]) * tap_of(row_y[:, None] - col_y[None])
    out = np.arange(ROWS)
    src = np.arange(3 * ROWS)
    full_x = ((src % CH)[None] == (out % CH)[:, None]) * tap_of((src // CH - BX)[None] - (out // CH)[:, None])
    return [jnp.asarray(m, BF16) for m in (pack, own_z, edges_z, full_y, full_x)]


def kernel(
    nx, ny, nz,
    live_ref, w_hbm, x_hbm, pack_hbm, ownz_hbm, edgez_hbm, fully_hbm, fullx_hbm,
    out_ref, tc_ref,
    wraw, src, wmap, xdat, pack, ownz, edgez, fully, fullx,
    zpack, fz, fyz, smooth, ze, ye, xe, grad, mixw, mixg, graw,
    cpart, rp, rx, c1, c2, etot, ep, ex,
    load_sem, hs, hr, ps, pr, xs, xr, gs, gr, eps, epr, exs, exr,
):
    ix, iy, iz = lax.axis_index("gx"), lax.axis_index("gy"), lax.axis_index("gz")
    lanes_y = T // ny
    rows_z = PR // nz
    plane = nz * ny
    cells = float(K * BX * BY * BZ * nx * ny * nz)

    loads = [
        pltpu.make_async_copy(a, b, load_sem.at[i])
        for i, (a, b) in enumerate(
            [(w_hbm, wraw), (pack_hbm, pack), (ownz_hbm, ownz), (edgez_hbm, edgez), (fully_hbm, fully),
             (fullx_hbm, fullx), (x_hbm, xdat)]
        )
    ]
    for load in loads:
        load.start()

    def plane_peers():
        for d in range(1, plane):
            yield d, lax.rem(iz + d // ny, nz), lax.rem(iy + d % ny, ny)

    def line_peers():
        for d in range(1, nx):
            yield d, lax.rem(ix + d, nx)

    barrier = pltpu.get_barrier_semaphore()
    for d, pz, py in plane_peers():
        pl.semaphore_signal(barrier, inc=1, device_id={"gz": pz, "gy": py}, device_id_type=MESH)
    for d, px in line_peers():
        pl.semaphore_signal(barrier, inc=1, device_id={"gx": px}, device_id_type=MESH)

    @pl.when(ix == 0)
    def _():
        xe[:, 0] = jnp.zeros_like(xe[:, 0])

    @pl.when(ix == nx - 1)
    def _():
        xe[:, 1] = jnp.zeros_like(xe[:, 1])

    @pl.when(iy == 0)
    def _():
        ye[:, :, :, : YZ // 2] = jnp.zeros_like(ye[:, :, :, : YZ // 2])

    @pl.when(iy == ny - 1)
    def _():
        ye[:, :, :, YZ // 2 :] = jnp.zeros_like(ye[:, :, :, YZ // 2 :])

    @pl.when(iz == 0)
    def _():
        ze[:, :, :, :128] = jnp.zeros_like(ze[:, :, :, :128])

    @pl.when(iz == nz - 1)
    def _():
        ze[:, :, :, 128:] = jnp.zeros_like(ze[:, :, :, 128:])

    loads[0].wait()
    for x in range(BX):
        wmap[x] = jnp.transpose(wraw[pl.ds(x * YZ, YZ), :])
        src[x] = wmap[x].astype(BF16)

    def dot(a, b):
        return jnp.dot(a, b, preferred_element_type=F32)

    def exact(a, b):
        return jnp.dot(a, b, precision=HIGH, preferred_element_type=F32)

    def remote(a, b, ssem, rsem, to):
        return pltpu.make_async_remote_copy(
            src_ref=a, dst_ref=b, send_sem=ssem, recv_sem=rsem, device_id=to, device_id_type=MESH
        )

    def maps(g):
        return pl.ds(g * CH, CH)

    def halo(s, g, axis):
        k, half = maps(g), YZ // 2
        if axis == "z":
            down = (0, zpack.at[:, k, pl.ds(0, 128)], ze.at[s, :, k, pl.ds(128, 128)])
            up = (1, zpack.at[:, k, pl.ds(128, 128)], ze.at[s, :, k, pl.ds(0, 128)])
            me, n = iz, nz
        elif axis == "y":
            down = (2, fz.at[:, k, pl.ds(0, half)], ye.at[s, :, k, pl.ds(half, half)])
            up = (3, fz.at[:, k, pl.ds(half, half)], ye.at[s, :, k, pl.ds(0, half)])
            me, n = iy, ny
        else:
            down = (4, fyz.at[:, k, :], xe.at[s, 1, :, k, :])
            up = (5, fyz.at[:, k, :], xe.at[s, 0, :, k, :])
            me, n = ix, nx

        def copy(i, a, b, to):
            return remote(a, b, hs.at[s, g, i], hr.at[s, g, i], {"g" + axis: to})

        return (
            (me > 0, me < n - 1, copy(*down, lax.rem(me + n - 1, n))),
            (me < n - 1, me > 0, copy(*up, lax.rem(me + 1, n))),
        )

    def send(s, g, axis):
        for sends, _, copy in halo(s, g, axis):
            @pl.when(sends)
            def _():
                copy.start()

    def receive(s, g, axis):
        for _, comes, copy in halo(s, g, axis):
            @pl.when(comes)
            def _():
                copy.wait_recv()

    def sent(s, g, axis):
        if s < 0:
            return
        for sends, _, copy in halo(s, g, axis):
            @pl.when(sends)
            def _():
                copy.wait_send()

    count = live_ref[0, 0, 0]
    row_y = lax.broadcasted_iota(jnp.int32, (1, YZ), 1) // BZ

    def mask_of(x):
        return x * BY + row_y < count

    def pack_z(s, g):
        k = maps(g)
        sent(s - 1, g, "z")
        zpack[:, k, :] = dot(src[:, k, :].reshape(ROWS, YZ), pack[...]).astype(BF16).reshape(BX, CH, 2 * 128)

    def send_z(s, g):
        send(s, g, "z")

    def filter_z(s, g):
        k = maps(g)
        sent(s - 1, g, "y")
        field = src[:, k, :].reshape(ROWS, YZ)
        own = jnp.concatenate([dot(field[:, : YZ // 2], ownz[...]), dot(field[:, YZ // 2 :], ownz[...])], axis=1)
        receive(s, g, "z")
        edges = dot(ze[s, :, k, :].reshape(ROWS, 2 * 128), edgez[...])
        fz[:, k, :] = (own + edges).astype(BF16).reshape(BX, CH, YZ)
        send(s, g, "y")

    def filter_y(s, g):
        k = maps(g)
        sent(s - 1, g, "x")
        receive(s, g, "y")
        field = jnp.concatenate([fz[:, k, :].reshape(ROWS, YZ), ye[s, :, k, :].reshape(ROWS, YZ)], axis=1)
        fyz[:, k, :] = dot(field, fully[...]).astype(BF16).reshape(BX, CH, YZ)
        send(s, g, "x")

    def filter_x(s, g):
        k = maps(g)
        receive(s, g, "x")
        field = jnp.concatenate(
            [xe[s, 0, :, k, :].reshape(ROWS, YZ), fyz[:, k, :].reshape(ROWS, YZ), xe[s, 1, :, k, :].reshape(ROWS, YZ)],
            axis=0,
        )
        return dot(fullx[...], field).reshape(BX, CH, YZ)

    def groups(p):
        return range(p * PAIR, (p + 1) * PAIR)

    def contribution(s, p):
        for g in groups(p):
            value = filter_x(s, g)
            for x in range(BX):
                smooth[x, maps(g), :] = jnp.where(mask_of(x), value[x], 0.0).astype(BF16)
        k = pl.ds(p * PR, PR)
        total = dot(smooth[0, k, :], xdat[pl.ds(0, YZ), :])
        for x in range(1, BX):
            total += dot(smooth[x, k, :], xdat[pl.ds(x * YZ, YZ), :])
        return total

    def gradient(p, courses):
        for x in range(BX):
            value = lax.dot_general(
                courses, xdat[pl.ds(x * YZ, YZ), :], (((1,), (1,)), ((), ())), preferred_element_type=F32
            )
            src[x, pl.ds(p * PR, PR), :] = jnp.where(mask_of(x), value, 0.0).astype(BF16)

    def square_sum(value):
        total = value[0] * value[0]
        for x in range(1, BX):
            total += value[x] * value[x]
        return jnp.sum(total)

    def piece(j_z, j_y):
        return pl.ds(pl.multiple_of(j_z * rows_z, rows_z), rows_z), pl.ds(pl.multiple_of(j_y * lanes_y, lanes_y), lanes_y)

    def height(a):
        return rows_z + 8 * a

    def reduce_start(a, g, value, energy):
        i = 2 * a + g
        for j in range(nz):
            cpart[i, j, :rows_z] = value[j * rows_z : (j + 1) * rows_z]
            if a:
                cpart[i, j, rows_z:] = jnp.full((8, T), energy, F32)
        for d, pz, py in plane_peers():
            reduce_copy(a, g, d, pz, py, iz * ny + iy).start()

    def reduce_copy(a, g, d, pz, py, slot):
        i, h = 2 * a + g, pl.ds(0, height(a))
        lanes = pl.ds(pl.multiple_of(py * lanes_y, lanes_y), lanes_y)
        return remote(
            cpart.at[i, pz, h, lanes], rp.at[i, slot, h], ps.at[i, d - 1], pr.at[i, slot], {"gz": pz, "gy": py}
        )

    def line_copy(a, g, d, px, slot):
        i, h = 2 * a + g, pl.ds(0, height(a))
        return remote(rx.at[i, nx, h], rx.at[i, slot, h], xs.at[i, d - 1], xr.at[i, slot], {"gx": px})

    def gather_copy(a, g, d, pz, py, z, y):
        i = 2 * a + g
        rows, lanes = piece(z, y)
        there = (c1, c2)[a].at[g, rows, lanes]
        return remote(there, there, gs.at[i, d - 1], gr.at[i, z * ny + y], {"gz": pz, "gy": py})

    def tree(parts):
        while len(parts) > 1:
            parts = [p + q for p, q in zip(parts[::2], parts[1::2])] + ([parts[-1]] if len(parts) % 2 else [])
        return parts[0]

    def reduce_line(a, g):
        i, h = 2 * a + g, height(a)
        for d, pz, py in plane_peers():
            reduce_copy(a, g, d, pz, py, pz * ny + py).wait_recv()
        lanes = pl.ds(pl.multiple_of(iy * lanes_y, lanes_y), lanes_y)
        rp[i, iz * ny + iy, :h] = cpart[i, iz, :h, lanes]
        rx[i, nx, :h] = tree([rp[i, j, :h] for j in range(plane)])
        for d, px in line_peers():
            line_copy(a, g, d, px, ix).start()

    def reduce_gather(a, g):
        i, h = 2 * a + g, height(a)
        for d, px in line_peers():
            line_copy(a, g, d, px, px).wait_recv()
        rx[i, ix, :h] = rx[i, nx, :h]
        total = tree([rx[i, j, :h] for j in range(nx)])
        rows, lanes = piece(iz, iy)
        (c1, c2)[a][g, rows, lanes] = total[:rows_z]
        if a:
            etot[g] = total[rows_z:]
        for d, pz, py in plane_peers():
            gather_copy(a, g, d, pz, py, iz, iy).start()

    def reduce_end(a, g):
        for d, pz, py in plane_peers():
            gather_copy(a, g, d, pz, py, pz, py).wait_recv()

    def gram_of(courses):
        gram = lax.dot_general(courses, courses, (((1,), (1,)), ((), ())), precision=HIGH, preferred_element_type=F32)
        diag = lax.broadcasted_iota(jnp.int32, (K, K), 0) == lax.broadcasted_iota(jnp.int32, (K, K), 1)
        return float(K) / jnp.sum(jnp.where(diag, gram, 0.0)) * gram

    known = {}

    def reduce_first(p):
        reduce_start(0, p, contribution(0, p), None)

    def first_gradient(p):
        reduce_end(0, p)
        gradient(p, c1[p].astype(BF16))
        for g in groups(p):
            pack_z(1, g)
            send_z(1, g)

    def second_source(g):
        value = filter_x(1, g)
        grad[:, maps(g), :] = value
        src[:, maps(g), :] = value.astype(BF16)
        pack_z(2, g)
        send_z(2, g)
        known["energy", g] = square_sum(value)

    def reduce_second(p):
        reduce_start(1, p, contribution(2, p), sum(known["energy", g] for g in groups(p)))

    def second_gradient(p):
        reduce_end(1, p)
        gradient(p, c2[p].astype(BF16))
        for g in groups(p):
            pack_z(3, g)
            send_z(3, g)

    def mix_maps():
        known["decay1"] = gram_of(c1[...].reshape(K, T))
        for x in range(BX):
            mixw[x] = wmap[x] - 0.5 * exact(known["decay1"], wmap[x])

    def mix_gradient():
        for x in range(BX):
            mixg[x] = grad[x] - 0.5 * exact(known["decay1"], grad[x])

    def second_courses():
        first = c1[...].reshape(K, T)
        scale = 1.0 / jnp.sqrt((etot[0, 0:1, 0:1] + etot[1, 0:1, 0:1]) / cells + 1e-06)
        known["scale1"] = scale
        courses = first + 0.5 * (scale * c2[...].reshape(K, T) - exact(known["decay1"], first))
        tc_ref[...] = courses.astype(BF16)
        decay = gram_of(courses)
        for x in range(BX):
            now = mixw[x] + 0.5 * scale * grad[x]
            out_ref[pl.ds(x * YZ, YZ), :] = jnp.transpose(now - 0.5 * exact(decay, now))

    def second_result(g):
        value = mixg[:, maps(g), :] + 0.5 * known["scale1"] * filter_x(3, g)
        mixg[:, maps(g), :] = value
        known["energy", g] = square_sum(value)

    every, pairs = range(NC), range(NP)
    loads[1].wait()
    for g in every:
        pack_z(0, g)
    pl.semaphore_wait(barrier, plane - 1 + nx - 1)
    for g in every:
        send_z(0, g)
    loads[2].wait()
    loads[3].wait()
    for g in every:
        filter_z(0, g)
    loads[4].wait()
    for g in every:
        filter_y(0, g)
    loads[5].wait()
    loads[6].wait()
    for step in (reduce_first, lambda p: reduce_line(0, p), lambda p: reduce_gather(0, p), first_gradient):
        for p in pairs:
            step(p)
    for g in every:
        filter_z(1, g)
    for g in every:
        filter_y(1, g)
    mix_maps()
    second_source(0)
    second_source(1)
    filter_z(2, 0)
    second_source(2)
    filter_z(2, 1)
    second_source(3)
    filter_y(2, 0)
    filter_z(2, 2)
    filter_y(2, 1)
    filter_z(2, 3)
    filter_y(2, 2)
    filter_y(2, 3)
    mix_gradient()
    for step in (reduce_second, lambda p: reduce_line(1, p), lambda p: reduce_gather(1, p), second_gradient):
        for p in pairs:
            step(p)
    for g in every:
        filter_z(3, g)
    for g in every:
        filter_y(3, g)
    second_courses()
    for g in every:
        second_result(g)
    me = iz * ny + iy
    ep[plane] = jnp.full((8, 128), sum(known["energy", g] for g in every), F32)

    def energy_plane(d, pz, py, slot):
        return remote(ep.at[plane], ep.at[slot], eps.at[d - 1], epr.at[slot], {"gz": pz, "gy": py})

    def energy_line(d, px, slot):
        return remote(ex.at[nx], ex.at[slot], exs.at[d - 1], exr.at[slot], {"gx": px})

    for d, pz, py in plane_peers():
        energy_plane(d, pz, py, me).start()
    for x in range(BX):
        graw[pl.ds(x * YZ, YZ), :] = jnp.transpose(mixg[x])
    for d, pz, py in plane_peers():
        energy_plane(d, pz, py, pz * ny + py).wait_recv()
    ep[me] = ep[plane]
    ex[nx] = tree([ep[j] for j in range(plane)])
    for d, px in line_peers():
        energy_line(d, px, ix).start()
    for g in every:
        for axis in "zyx":
            sent(3, g, axis)
    for a in (0, 1):
        for g in pairs:
            for d, pz, py in plane_peers():
                reduce_copy(a, g, d, pz, py, me).wait_send()
                gather_copy(a, g, d, pz, py, iz, iy).wait_send()
            for d, px in line_peers():
                line_copy(a, g, d, px, ix).wait_send()
    for d, pz, py in plane_peers():
        energy_plane(d, pz, py, me).wait_send()
    for d, px in line_peers():
        energy_line(d, px, px).wait_recv()
    ex[ix] = ex[nx]
    total = tree([ex[j] for j in range(nx)])
    half_scale = 0.5 / jnp.sqrt(total[0:1, 0:1] / cells + 1e-06)
    for x in range(BX):
        rows = pl.ds(x * YZ, YZ)
        out_ref[rows, :] = out_ref[rows, :] + half_scale * graw[rows, :]
    for d, px in line_peers():
        energy_line(d, px, ix).wait_send()


def per_device(nx, ny, nz, bold_data, spatial_maps, live_blocks):
    rows_z, lanes_y, plane = PR // nz, T // ny, ny * nz
    voxels = jnp.transpose(spatial_maps, (1, 2, 3, 0)).reshape(BX * YZ, K)
    matrices = filter_matrices()
    vmem, dma = pltpu.VMEM, pltpu.SemaphoreType.DMA
    field, wide, raw = vmem((BX, K, YZ), BF16), vmem((BX, K, YZ), F32), vmem((BX * YZ, K), F32)
    new_maps, courses = pl.pallas_call(
        functools.partial(kernel, nx, ny, nz),
        out_shape=(jax.ShapeDtypeStruct((BX * YZ, K), F32), jax.ShapeDtypeStruct((K, T), BF16)),
        in_specs=[pl.BlockSpec(memory_space=pltpu.SMEM)] + [pl.BlockSpec(memory_space=pl.ANY)] * 7,
        out_specs=(pl.BlockSpec(memory_space=pltpu.VMEM), pl.BlockSpec(memory_space=pltpu.VMEM)),
        scratch_shapes=[
            raw, field, wide, vmem((BX * YZ, T), BF16),
            *[vmem(m.shape, BF16) for m in matrices],
            vmem((BX, K, 256), BF16), field, field, field,
            vmem((4, BX, K, 256), BF16), vmem((4, BX, K, YZ), BF16), vmem((4, 2, BX, K, YZ), BF16),
            wide, wide, wide, raw,
            vmem((4, nz, rows_z + 8, T), F32), vmem((4, plane, rows_z + 8, lanes_y), F32),
            vmem((4, nx + 1, rows_z + 8, lanes_y), F32),
            vmem((NP, PR, T), F32), vmem((NP, PR, T), F32), vmem((NP, 8, lanes_y), F32),
            vmem((plane + 1, 8, 128), F32), vmem((nx + 1, 8, 128), F32),
            dma((7,)), dma((4, NC, 6)), dma((4, NC, 6)),
            dma((4, plane)), dma((4, plane)), dma((4, nx)), dma((4, nx)), dma((4, plane)), dma((4, plane)),
            dma((plane,)), dma((plane,)), dma((nx,)), dma((nx,)),
        ],
        compiler_params=pltpu.CompilerParams(
            collective_id=0, has_side_effects=True, vmem_limit_bytes=56 * 1024 * 1024
        ),
    )(live_blocks, voxels, bold_data.reshape(BX * YZ, T), *matrices)
    new_maps = jnp.transpose(new_maps.reshape(BX, BY, BZ, K), (3, 0, 1, 2))
    return new_maps, courses


def solution(mesh):
    return jax.shard_map(
        functools.partial(per_device, mesh.shape["gx"], mesh.shape["gy"], mesh.shape["gz"]),
        mesh=mesh,
        in_specs=(P("gx", "gy", "gz", None), P(None, "gx", "gy", "gz"), P("gx", "gy", "gz")),
        out_specs=(P(None, "gx", "gy", "gz"), P()),
        check_vma=False,
    )
```

```python
import functools
import math

import jax
import jax.numpy as jnp
import numpy as np
from jax import lax
from jax.experimental import pallas as pl
from jax.experimental.pallas import tpu as pltpu
from jax.sharding import PartitionSpec as P

MESH = pl.DeviceIdType.MESH
RADIUS = 8
K, T = 64, 512
BX, BY, BZ = 8, 16, 32
YZ = BY * BZ
CH = 16
NC = K // CH
PAIR = 2
PR, NP = PAIR * CH, NC // PAIR
ROWS = BX * CH
F32, BF16 = jnp.float32, jnp.bfloat16
HIGH = lax.Precision.HIGHEST


def tap_of(offset):
    total = sum(math.exp(-float(d * d) / 32.0) for d in range(-RADIUS, RADIUS + 1))
    taps = np.exp(-np.square(np.asarray(offset, np.float64)) / 32.0) / total
    return np.where(np.abs(offset) <= RADIUS, taps, 0.0)


def filter_matrices():
    col = np.arange(YZ)
    col_y, col_z = col // BZ, col % BZ
    edge = np.arange(2 * BY * RADIUS)
    edge_y = (edge % (BY * RADIUS)) // RADIUS
    low = edge < BY * RADIUS
    edge_z = np.where(low, edge % RADIUS, BZ - RADIUS + edge % RADIUS)
    pack = (col_y[:, None] == edge_y[None]) & (col_z[:, None] == edge_z[None])
    near = np.arange(BY * RADIUS) // RADIUS
    corner = np.arange(4 * RADIUS * RADIUS)
    corner_y = (corner % RADIUS**2) // RADIUS + np.where(corner // RADIUS**2 % 2 == 0, -RADIUS, BY)
    corner_z = corner % RADIUS + np.where(corner < 2 * RADIUS**2, -RADIUS, BZ)
    half = col[: YZ // 2]
    row_y = np.concatenate([col_y, half // BZ - RADIUS, half // BZ + BY, near, near, corner_y])
    row_z = np.concatenate([col_z, half % BZ, half % BZ, edge % RADIUS + np.where(low, -RADIUS, BZ), corner_z])
    full_yz = tap_of(row_y[:, None] - col_y[None]) * tap_of(row_z[:, None] - col_z[None])
    out = np.arange(ROWS)
    src = np.arange(3 * ROWS)
    full_x = ((src % CH)[None] == (out % CH)[:, None]) * tap_of((src // CH - BX)[None] - (out // CH)[:, None])
    return [jnp.asarray(m, BF16) for m in (pack, full_yz, full_x)]


def kernel(
    nx, ny, nz,
    live_ref, w_hbm, x_hbm, pack_hbm, full_hbm, fullx_hbm,
    out_ref, tc_ref,
    wraw, src, wmap, xdat, pack, full, fullx,
    zpack, cpack, fyz, smooth, ze, ye, ce, xe, grad, mixw, mixg, graw,
    cpart, rp, rx, c1, c2, etot, ep, ex,
    load_sem, hs, hr, ps, pr, xs, xr, gs, gr, eps, epr, exs, exr,
):
    ix, iy, iz = lax.axis_index("gx"), lax.axis_index("gy"), lax.axis_index("gz")
    lanes_y = T // ny
    rows_z = PR // nz
    plane = nz * ny
    cells = float(K * BX * BY * BZ * nx * ny * nz)

    loads = [
        pltpu.make_async_copy(a, b, load_sem.at[i])
        for i, (a, b) in enumerate([(w_hbm, wraw), (pack_hbm, pack), (full_hbm, full), (fullx_hbm, fullx), (x_hbm, xdat)])
    ]
    loads[0].start()
    loads[1].start()

    def plane_peers():
        for d in range(1, plane):
            yield d, lax.rem(iz + d // ny, nz), lax.rem(iy + d % ny, ny)

    def line_peers():
        for d in range(1, nx):
            yield d, lax.rem(ix + d, nx)

    barrier = pltpu.get_barrier_semaphore()
    for d, pz, py in plane_peers():
        pl.semaphore_signal(barrier, inc=1, device_id={"gz": pz, "gy": py}, device_id_type=MESH)
    for d, px in line_peers():
        pl.semaphore_signal(barrier, inc=1, device_id={"gx": px}, device_id_type=MESH)

    @pl.when(ix == 0)
    def _():
        xe[:, 0] = jnp.zeros_like(xe[:, 0])

    @pl.when(ix == nx - 1)
    def _():
        xe[:, 1] = jnp.zeros_like(xe[:, 1])

    @pl.when(iy == 0)
    def _():
        ye[:, :, :, : YZ // 2] = jnp.zeros_like(ye[:, :, :, : YZ // 2])

    @pl.when(iy == ny - 1)
    def _():
        ye[:, :, :, YZ // 2 :] = jnp.zeros_like(ye[:, :, :, YZ // 2 :])

    @pl.when(iz == 0)
    def _():
        ze[:, :, :, :128] = jnp.zeros_like(ze[:, :, :, :128])

    @pl.when(iz == nz - 1)
    def _():
        ze[:, :, :, 128:] = jnp.zeros_like(ze[:, :, :, 128:])

    for i, (gone_y, gone_z) in enumerate(((0, 0), (ny - 1, 0), (0, nz - 1), (ny - 1, nz - 1))):
        @pl.when((iy == gone_y) | (iz == gone_z))
        def _():
            ce[:, i] = jnp.zeros_like(ce[:, i])

    loads[0].wait()
    for load in loads[2:]:
        load.start()

    @pl.loop(0, BX)
    def _(x):
        wmap[x] = jnp.transpose(wraw[pl.ds(pl.multiple_of(x * YZ, YZ), YZ), :])
        src[x] = wmap[x].astype(BF16)


    def dot(a, b):
        return jnp.dot(a, b, preferred_element_type=F32)

    def exact(a, b):
        return jnp.dot(a, b, precision=HIGH, preferred_element_type=F32)

    def remote(a, b, ssem, rsem, to):
        return pltpu.make_async_remote_copy(
            src_ref=a, dst_ref=b, send_sem=ssem, recv_sem=rsem, device_id=to, device_id_type=MESH
        )

    def maps(g):
        return pl.ds(g * CH, CH)

    def halo(s, g, axis):
        k, half = maps(g), YZ // 2
        up_y, down_y = lax.rem(iy + 1, ny), lax.rem(iy + ny - 1, ny)
        up_z, down_z = lax.rem(iz + 1, nz), lax.rem(iz + nz - 1, nz)
        low_y, high_y, low_z, high_z = iy > 0, iy < ny - 1, iz > 0, iz < nz - 1

        def copy(i, a, b, to):
            return remote(a, b, hs.at[s, g, i], hr.at[s, g, i], to)

        if axis == "z":
            return (
                (low_z, high_z, copy(0, zpack.at[:, k, pl.ds(0, 128)], ze.at[s, :, k, pl.ds(128, 128)], {"gz": down_z})),
                (high_z, low_z, copy(1, zpack.at[:, k, pl.ds(128, 128)], ze.at[s, :, k, pl.ds(0, 128)], {"gz": up_z})),
            )
        if axis == "y":
            return (
                (low_y, high_y, copy(2, src.at[:, k, pl.ds(0, half)], ye.at[s, :, k, pl.ds(half, half)], {"gy": down_y})),
                (high_y, low_y, copy(3, src.at[:, k, pl.ds(half, half)], ye.at[s, :, k, pl.ds(0, half)], {"gy": up_y})),
            )
        if axis == "c":
            ways = (
                (high_y & high_z, low_y & low_z, up_y, up_z), (low_y & high_z, high_y & low_z, down_y, up_z),
                (high_y & low_z, low_y & high_z, up_y, down_z), (low_y & low_z, high_y & high_z, down_y, down_z),
            )
            return tuple(
                (sends, comes, copy(6 + i, cpack.at[i, :, k, :], ce.at[s, i, :, k, :], {"gy": to_y, "gz": to_z}))
                for i, (sends, comes, to_y, to_z) in enumerate(ways)
            )
        down_x, up_x = lax.rem(ix + nx - 1, nx), lax.rem(ix + 1, nx)
        return (
            (ix > 0, ix < nx - 1, copy(4, fyz.at[:, k, :], xe.at[s, 1, :, k, :], {"gx": down_x})),
            (ix < nx - 1, ix > 0, copy(5, fyz.at[:, k, :], xe.at[s, 0, :, k, :], {"gx": up_x})),
        )

    def send(s, g, axis):
        for sends, _, copy in halo(s, g, axis):
            @pl.when(sends)
            def _():
                copy.start()

    def receive(s, g, axis):
        for _, comes, copy in halo(s, g, axis):
            @pl.when(comes)
            def _():
                copy.wait_recv()

    def sent(s, g, axis):
        if s < 0:
            return
        for sends, _, copy in halo(s, g, axis):
            @pl.when(sends)
            def _():
                copy.wait_send()

    count = live_ref[0, 0, 0]
    row_y = lax.broadcasted_iota(jnp.int32, (1, YZ), 1) // BZ

    def mask_of(x):
        return x * BY + row_y < count

    first_half = lax.broadcasted_iota(jnp.int32, (ROWS // 2, 128), 1) < 64

    def joined(a, b):
        return jnp.where(first_half, a, pltpu.roll(b, 64, 1)), jnp.where(first_half, pltpu.roll(a, 64, 1), b)

    def pack_z(s, g):
        k = maps(g)
        sent(s - 1, g, "z")
        sent(s - 1, g, "c")
        edges = dot(src[:, k, :].reshape(ROWS, YZ), pack[...])
        zpack[:, k, :] = edges.astype(BF16).reshape(BX, CH, 2 * 128)
        for i, lanes in ((2, slice(0, 128)), (0, slice(128, 256))):
            low, high = joined(edges[: ROWS // 2, lanes], edges[ROWS // 2 :, lanes])
            cpack[i, :, k, :] = high.astype(BF16).reshape(BX // 2, CH, 128)
            cpack[i + 1, :, k, :] = low.astype(BF16).reshape(BX // 2, CH, 128)

    def send_z(s, g):
        send(s, g, "y")
        send(s, g, "c")
        send(s, g, "z")

    def filter_yz(s, g):
        k = maps(g)
        sent(s - 1, g, "x")
        own = dot(src[:, k, :].reshape(ROWS, YZ), full[pl.ds(0, YZ), :])
        for axis in "zyc":
            receive(s, g, axis)
        corners = [ce[s, i, :, k, :].reshape(ROWS // 2, 128).astype(F32) for i in range(4)]
        low, high = joined(*corners[:2]), joined(*corners[2:])
        corners = jnp.concatenate(
            [jnp.concatenate([low[0], high[0]], axis=1), jnp.concatenate([low[1], high[1]], axis=1)], axis=0
        ).astype(BF16)
        field = jnp.concatenate([ye[s, :, k, :].reshape(ROWS, YZ), ze[s, :, k, :].reshape(ROWS, 2 * 128), corners], axis=1)
        fyz[:, k, :] = (own + dot(field, full[pl.ds(YZ, 2 * YZ), :])).astype(BF16).reshape(BX, CH, YZ)
        send(s, g, "x")

    def filter_x(s, g):
        k = maps(g)
        receive(s, g, "x")
        field = jnp.concatenate(
            [xe[s, 0, :, k, :].reshape(ROWS, YZ), fyz[:, k, :].reshape(ROWS, YZ), xe[s, 1, :, k, :].reshape(ROWS, YZ)],
            axis=0,
        )
        return dot(fullx[...], field).reshape(BX, CH, YZ)

    def groups(p):
        return range(p * PAIR, (p + 1) * PAIR)

    def contribution(s, p):
        for g in groups(p):
            value = filter_x(s, g)
            for x in range(BX):
                smooth[x, maps(g), :] = jnp.where(mask_of(x), value[x], 0.0).astype(BF16)
        k = pl.ds(p * PR, PR)
        total = dot(smooth[0, k, :], xdat[pl.ds(0, YZ), :])
        for x in range(1, BX):
            total += dot(smooth[x, k, :], xdat[pl.ds(x * YZ, YZ), :])
        return total

    def gradient(s, p, courses):
        for g in groups(p):
            sent(s - 1, g, "y")
        for x in range(BX):
            value = lax.dot_general(
                courses, xdat[pl.ds(x * YZ, YZ), :], (((1,), (1,)), ((), ())), preferred_element_type=F32
            )
            src[x, pl.ds(p * PR, PR), :] = jnp.where(mask_of(x), value, 0.0).astype(BF16)

    def square_sum(value):
        total = value[0] * value[0]
        for x in range(1, BX):
            total += value[x] * value[x]
        return jnp.sum(total)

    def piece(j_z, j_y):
        return pl.ds(pl.multiple_of(j_z * rows_z, rows_z), rows_z), pl.ds(pl.multiple_of(j_y * lanes_y, lanes_y), lanes_y)

    def height(a):
        return rows_z + 8 * a

    def reduce_start(a, g, value, energy):
        i = 2 * a + g
        for j in range(nz):
            cpart[i, j, :rows_z] = value[j * rows_z : (j + 1) * rows_z]
            if a:
                cpart[i, j, rows_z:] = jnp.full((8, T), energy, F32)
        for d, pz, py in plane_peers():
            reduce_copy(a, g, d, pz, py, iz * ny + iy).start()

    def reduce_copy(a, g, d, pz, py, slot):
        i, h = 2 * a + g, pl.ds(0, height(a))
        lanes = pl.ds(pl.multiple_of(py * lanes_y, lanes_y), lanes_y)
        return remote(
            cpart.at[i, pz, h, lanes], rp.at[i, slot, h], ps.at[i, d - 1], pr.at[i, slot], {"gz": pz, "gy": py}
        )

    def line_copy(a, g, d, px, slot):
        i, h = 2 * a + g, pl.ds(0, height(a))
        return remote(rx.at[i, nx, h], rx.at[i, slot, h], xs.at[i, d - 1], xr.at[i, slot], {"gx": px})

    def gather_copy(a, g, d, pz, py, z, y):
        i = 2 * a + g
        rows, lanes = piece(z, y)
        there = (c1, c2)[a].at[g, rows, lanes]
        return remote(there, there, gs.at[i, d - 1], gr.at[i, z * ny + y], {"gz": pz, "gy": py})

    def tree(parts):
        while len(parts) > 1:
            parts = [p + q for p, q in zip(parts[::2], parts[1::2])] + ([parts[-1]] if len(parts) % 2 else [])
        return parts[0]

    def reduce_line(a, g):
        i, h = 2 * a + g, height(a)
        for d, pz, py in plane_peers():
            reduce_copy(a, g, d, pz, py, pz * ny + py).wait_recv()
        lanes = pl.ds(pl.multiple_of(iy * lanes_y, lanes_y), lanes_y)
        rp[i, iz * ny + iy, :h] = cpart[i, iz, :h, lanes]
        rx[i, nx, :h] = tree([rp[i, j, :h] for j in range(plane)])
        for d, px in line_peers():
            line_copy(a, g, d, px, ix).start()

    def reduce_gather(a, g):
        i, h = 2 * a + g, height(a)
        for d, px in line_peers():
            line_copy(a, g, d, px, px).wait_recv()
        rx[i, ix, :h] = rx[i, nx, :h]
        total = tree([rx[i, j, :h] for j in range(nx)])
        rows, lanes = piece(iz, iy)
        (c1, c2)[a][g, rows, lanes] = total[:rows_z]
        if a:
            etot[g] = total[rows_z:]
        for d, pz, py in plane_peers():
            gather_copy(a, g, d, pz, py, iz, iy).start()

    def reduce_end(a, g):
        for d, pz, py in plane_peers():
            gather_copy(a, g, d, pz, py, pz, py).wait_recv()

    def gram_of(courses):
        gram = lax.dot_general(courses, courses, (((1,), (1,)), ((), ())), precision=HIGH, preferred_element_type=F32)
        diag = lax.broadcasted_iota(jnp.int32, (K, K), 0) == lax.broadcasted_iota(jnp.int32, (K, K), 1)
        return float(K) / jnp.sum(jnp.where(diag, gram, 0.0)) * gram

    known = {}

    def reduce_first(p):
        reduce_start(0, p, contribution(0, p), None)

    def first_gradient(p):
        reduce_end(0, p)
        gradient(1, p, c1[p].astype(BF16))
        for g in groups(p):
            pack_z(1, g)
            send_z(1, g)

    def second_source(g):
        value = filter_x(1, g)
        sent(1, g, "y")
        grad[:, maps(g), :] = value
        src[:, maps(g), :] = value.astype(BF16)
        pack_z(2, g)
        send_z(2, g)
        known["energy", g] = square_sum(value)

    def reduce_second(p):
        reduce_start(1, p, contribution(2, p), sum(known["energy", g] for g in groups(p)))

    def second_gradient(p):
        reduce_end(1, p)
        gradient(3, p, c2[p].astype(BF16))
        for g in groups(p):
            pack_z(3, g)
            send_z(3, g)

    def mix_maps():
        known["decay1"] = gram_of(c1[...].reshape(K, T))
        @pl.loop(0, BX)
        def _(x):
            mixw[x] = wmap[x] - 0.5 * exact(known["decay1"], wmap[x])

    def mix_gradient():
        @pl.loop(0, BX)
        def _(x):
            mixg[x] = grad[x] - 0.5 * exact(known["decay1"], grad[x])

    def second_courses():
        first = c1[...].reshape(K, T)
        scale = 1.0 / jnp.sqrt((etot[0, 0:1, 0:1] + etot[1, 0:1, 0:1]) / cells + 1e-06)
        known["scale1"] = scale
        courses = first + 0.5 * (scale * c2[...].reshape(K, T) - exact(known["decay1"], first))
        tc_ref[...] = courses.astype(BF16)
        decay = gram_of(courses)

        @pl.loop(0, BX)
        def _(x):
            now = mixw[x] + 0.5 * scale * grad[x]
            out_ref[pl.ds(pl.multiple_of(x * YZ, YZ), YZ), :] = jnp.transpose(now - 0.5 * exact(decay, now))

    def second_result(g):
        value = mixg[:, maps(g), :] + 0.5 * known["scale1"] * filter_x(3, g)
        mixg[:, maps(g), :] = value
        known["energy", g] = square_sum(value)

    every, pairs = range(NC), range(NP)
    loads[1].wait()
    for g in every:
        pack_z(0, g)
    pl.semaphore_wait(barrier, plane - 1 + nx - 1)
    for g in every:
        send_z(0, g)
    loads[2].wait()
    for g in every:
        filter_yz(0, g)
    loads[3].wait()
    loads[4].wait()
    for step in (reduce_first, lambda p: reduce_line(0, p), lambda p: reduce_gather(0, p), first_gradient):
        for p in pairs:
            step(p)
    for g in every:
        filter_yz(1, g)
    mix_maps()
    second_source(0)
    second_source(1)
    filter_yz(2, 0)
    second_source(2)
    filter_yz(2, 1)
    second_source(3)
    filter_yz(2, 2)
    filter_yz(2, 3)
    mix_gradient()
    for step in (reduce_second, lambda p: reduce_line(1, p), lambda p: reduce_gather(1, p), second_gradient):
        for p in pairs:
            step(p)
    for g in every:
        filter_yz(3, g)
    second_courses()
    for g in every:
        second_result(g)
    me = iz * ny + iy
    ep[plane] = jnp.full((8, 128), sum(known["energy", g] for g in every), F32)

    def energy_plane(d, pz, py, slot):
        return remote(ep.at[plane], ep.at[slot], eps.at[d - 1], epr.at[slot], {"gz": pz, "gy": py})

    def energy_line(d, px, slot):
        return remote(ex.at[nx], ex.at[slot], exs.at[d - 1], exr.at[slot], {"gx": px})

    for d, pz, py in plane_peers():
        energy_plane(d, pz, py, me).start()

    @pl.loop(0, BX)
    def _(x):
        graw[pl.ds(pl.multiple_of(x * YZ, YZ), YZ), :] = jnp.transpose(mixg[x])

    for d, pz, py in plane_peers():
        energy_plane(d, pz, py, pz * ny + py).wait_recv()
    ep[me] = ep[plane]
    ex[nx] = tree([ep[j] for j in range(plane)])
    for d, px in line_peers():
        energy_line(d, px, ix).start()
    for g in every:
        for axis in "zycx":
            sent(3, g, axis)
    for a in (0, 1):
        for g in pairs:
            for d, pz, py in plane_peers():
                reduce_copy(a, g, d, pz, py, me).wait_send()
                gather_copy(a, g, d, pz, py, iz, iy).wait_send()
            for d, px in line_peers():
                line_copy(a, g, d, px, ix).wait_send()
    for d, pz, py in plane_peers():
        energy_plane(d, pz, py, me).wait_send()
    for d, px in line_peers():
        energy_line(d, px, px).wait_recv()
    ex[ix] = ex[nx]
    total = tree([ex[j] for j in range(nx)])
    half_scale = 0.5 / jnp.sqrt(total[0:1, 0:1] / cells + 1e-06)
    for x in range(BX):
        rows = pl.ds(x * YZ, YZ)
        out_ref[rows, :] = out_ref[rows, :] + half_scale * graw[rows, :]
    for d, px in line_peers():
        energy_line(d, px, ix).wait_send()


def per_device(nx, ny, nz, bold_data, spatial_maps, live_blocks):
    rows_z, lanes_y, plane = PR // nz, T // ny, ny * nz
    voxels = jnp.transpose(spatial_maps, (1, 2, 3, 0)).reshape(BX * YZ, K)
    matrices = filter_matrices()
    vmem, dma = pltpu.VMEM, pltpu.SemaphoreType.DMA
    field, wide, raw = vmem((BX, K, YZ), BF16), vmem((BX, K, YZ), F32), vmem((BX * YZ, K), F32)
    new_maps, courses = pl.pallas_call(
        functools.partial(kernel, nx, ny, nz),
        out_shape=(jax.ShapeDtypeStruct((BX * YZ, K), F32), jax.ShapeDtypeStruct((K, T), BF16)),
        in_specs=[pl.BlockSpec(memory_space=pltpu.SMEM)] + [pl.BlockSpec(memory_space=pl.ANY)] * 5,
        out_specs=(pl.BlockSpec(memory_space=pltpu.VMEM), pl.BlockSpec(memory_space=pltpu.VMEM)),
        scratch_shapes=[
            raw, field, wide, vmem((BX * YZ, T), BF16),
            *[vmem(m.shape, BF16) for m in matrices],
            vmem((BX, K, 256), BF16), vmem((4, BX // 2, K, 128), BF16), field, field,
            vmem((4, BX, K, 256), BF16), vmem((4, BX, K, YZ), BF16), vmem((4, 4, BX // 2, K, 128), BF16),
            vmem((4, 2, BX, K, YZ), BF16),
            wide, wide, wide, raw,
            vmem((4, nz, rows_z + 8, T), F32), vmem((4, plane, rows_z + 8, lanes_y), F32),
            vmem((4, nx + 1, rows_z + 8, lanes_y), F32),
            vmem((NP, PR, T), F32), vmem((NP, PR, T), F32), vmem((NP, 8, lanes_y), F32),
            vmem((plane + 1, 8, 128), F32), vmem((nx + 1, 8, 128), F32),
            dma((5,)), dma((4, NC, 10)), dma((4, NC, 10)),
            dma((4, plane)), dma((4, plane)), dma((4, nx)), dma((4, nx)), dma((4, plane)), dma((4, plane)),
            dma((plane,)), dma((plane,)), dma((nx,)), dma((nx,)),
        ],
        compiler_params=pltpu.CompilerParams(
            collective_id=0, has_side_effects=True, vmem_limit_bytes=56 * 1024 * 1024
        ),
    )(live_blocks, voxels, bold_data.reshape(BX * YZ, T), *matrices)
    new_maps = jnp.transpose(new_maps.reshape(BX, BY, BZ, K), (3, 0, 1, 2))
    return new_maps, courses


def solution(mesh):
    return jax.shard_map(
        functools.partial(per_device, mesh.shape["gx"], mesh.shape["gy"], mesh.shape["gz"]),
        mesh=mesh,
        in_specs=(P("gx", "gy", "gz", None), P(None, "gx", "gy", "gz"), P("gx", "gy", "gz")),
        out_specs=(P(None, "gx", "gy", "gz"), P()),
        check_vma=False,
    )
```
